32 devices in a mesh: vis: 4 (over y, core), row: 4 (over z), col: 2 (over x).
Axes of the slice: x: 2, y: 2, z: 4, core: 2. Of those that a mesh axis runs over, the one named last changes fastest.
Arguments:
- images: bfloat16 [128, 6400], P(('vis', 'row', 'col')), may hold values from -6 to 6
- counts: int32 [4], replicated, may hold values from 1 to 32, 64 in all
- block_order: int32 [4], replicated, may hold values from 0 to 3, each once
- projector_norm_gain: float32 [6400], replicated, may hold values from 0.1 to 1.9
- proj_first: bfloat16 [6400, 4096], P('vis', ('row', 'col')), may hold values from -0.078125 to 0.078125
- proj_bias: float32 [4096], P(('row', 'col')), may hold values from -3 to 3
- proj_second: bfloat16 [4096, 4096], P(('row', 'col'), 'vis'), may hold values from -0.09375 to 0.09375
- gate_weight: bfloat16 [4096, 16384], P('vis', ('row', 'col')), may hold values from -0.09375 to 0.09375
- up_weight: bfloat16 [4096, 16384], P('vis', ('row', 'col')), may hold values from -0.09375 to 0.09375
- down_weight: bfloat16 [16384, 4096], P(('row', 'col'), 'vis'), may hold values from -0.046875 to 0.046875
- cotangent: bfloat16 [64, 4096], P(('row', 'col'), 'vis'), may hold values from -6 to 6
Outputs:
- block_out: bfloat16 [64, 4096], P(('row', 'col'), 'vis')
- image_slot_gradients: float32 [128, 6400], P(('vis', 'row', 'col'))
- first_grad: float32 [6400, 4096], P('vis', ('row', 'col'))
- second_grad: float32 [4096, 4096], P(('row', 'col'), 'vis')
The draws below stay inside these ranges and needn't reach their ends.
Inputs may be any that keep to these rules, and one draw needn't show every extreme that they name: Vision device v's live rows are its first counts[v] slots; the counts sum to 64, and some device's slots are all live. `block_order`: each vision device's index once: the order in which the devices' live rows follow one another among the language rows.
All inputs are finite; a program needn't handle non-finite values.
Results may differ from the reference program's by a relative error of at most 0.034.
Values may be sent and summed in bfloat16 or wider, within the bound.
A program may use at most 64 MiB of HBM per device.

```python
import math
import jax
import jax.numpy as jnp
import numpy as np
from jax import lax

VIT = 6400
PROJ = 4096
D = 4096
FF = 16384
CAP = 32
ROWS = 64
N_VIS = 4


def shard_levels(stream_key, shape, pieces, low, largest):
    level = 1.0
    for dim, shards_of in pieces:
        heights = jax.random.uniform(jax.random.fold_in(jax.random.fold_in(stream_key, 6), dim), (shards_of,), jnp.float32, low / len(pieces), largest / len(pieces))
        level = level * jnp.repeat(jnp.exp(heights), shape[dim] // shards_of).reshape((-1,) + (1,) * (len(shape) - 1 - dim))
    return level


def length_profile(number_of, total, reach, lean):
    loads = [(1 << 20) // math.isqrt(grade ** lean) + 1 for grade in range(2, number_of + 1)]
    spare, given = total - reach - (number_of - 1), [1] * (number_of - 1)
    while spare > 0:
        free = [i for i in range(number_of - 1) if given[i] < reach]
        whole, left = sum([loads[i] for i in free]), spare
        for i in free:
            more = min(reach - given[i], max(1, left * loads[i] // whole), spare)
            given[i] = given[i] + more
            spare = spare - more
    return np.array([reach] + given)


def ragged(stream_key, amount, total, reach, skew):
    if amount == 2:
        one = jax.random.randint(stream_key, (), max(1, total - reach), min(reach, total - 1) + 1)
        return jnp.stack([one, total - one])
    lengths = jnp.asarray(length_profile(amount, total, reach, skew), jnp.int32)
    pairs = (amount - 1) // 2
    source_of, taker = lengths[1:1 + 2 * pairs:2], lengths[2:2 + 2 * pairs:2]
    margin = jnp.minimum(source_of - 1, reach - taker)
    passed = jax.random.randint(jax.random.fold_in(stream_key, 1), (pairs,), 0, 1 << 20) % (margin + 1)
    lengths = lengths.at[1:1 + 2 * pairs:2].set(source_of - passed).at[2:2 + 2 * pairs:2].set(taker + passed)
    return lengths[jax.random.permutation(jax.random.fold_in(stream_key, 2), amount)]


def noise(stream_key, shape, spread, limit, split=(), kind=jnp.bfloat16):
    gain = shard_levels(stream_key, shape, split, -0.22, 0.18) if split else 1.0
    result = jax.random.normal(stream_key, shape, jnp.float32) * spread * gain
    return jnp.minimum(jnp.maximum(result, -limit), limit).astype(kind)


def setup_inputs(seed: int = 0) -> dict:
    key_list = jax.random.split(jax.random.key(seed), 12)
    images = noise(key_list[0], (N_VIS * CAP, VIT), 1.0, 6.0, ((0, 32),))
    counts = ragged(key_list[1], N_VIS, ROWS, CAP, 2).astype(jnp.int32)
    block_order = jax.random.permutation(key_list[2], N_VIS).astype(jnp.int32)
    projector_norm_gain = jnp.clip(1.0 + 0.18 * jax.random.normal(key_list[3], (VIT,), jnp.float32), 0.1, 1.9)
    proj_first = noise(key_list[4], (VIT, PROJ), VIT ** -0.5, 0.078125, ((0, 4), (1, 8)))
    proj_bias = noise(key_list[5], (PROJ,), 0.5, 3.0, ((0, 8),), jnp.float32)
    proj_second = noise(key_list[6], (PROJ, D), PROJ ** -0.5, 0.09375, ((0, 8), (1, 4)))
    gate_weight = noise(key_list[7], (D, FF), D ** -0.5, 0.09375, ((0, 4), (1, 8)))
    up_weight = noise(key_list[8], (D, FF), D ** -0.5, 0.09375, ((0, 4), (1, 8)))
    down_weight = noise(key_list[9], (FF, D), FF ** -0.5, 0.046875, ((0, 8), (1, 4)))
    cotangent = noise(key_list[10], (ROWS, D), 1.0, 6.0, ((0, 8), (1, 4)))
    return dict(images=images, counts=counts, block_order=block_order, projector_norm_gain=projector_norm_gain, proj_first=proj_first, proj_bias=proj_bias, proj_second=proj_second, gate_weight=gate_weight, up_weight=up_weight, down_weight=down_weight, cotangent=cotangent)


def row_tables(counts, block_order, total_rows, per_device, group_size):
    vision = counts.shape[0]
    labels = jnp.arange(vision, dtype=jnp.int32)
    chosen = (block_order[:, None] == labels[None, :]).astype(jnp.int32)
    ordered = lax.optimization_barrier(jnp.sum(chosen * counts[None, :], axis=1)).astype(jnp.int32)
    block_ends = jnp.cumsum(ordered).astype(jnp.int32)
    block_starts = (block_ends - ordered).astype(jnp.int32)
    language = jnp.arange(total_rows, dtype=jnp.int32)
    block_of = lax.optimization_barrier(jnp.sum((block_ends[None, :] <= language[:, None]).astype(jnp.int32), axis=1)).astype(jnp.int32)
    picked = (block_of[:, None] == labels[None, :]).astype(jnp.int32)
    owner = lax.optimization_barrier(jnp.sum(picked * block_order[None, :], axis=1)).astype(jnp.int32)
    offset = (language - lax.optimization_barrier(jnp.sum(picked * block_starts[None, :], axis=1))).astype(jnp.int32)
    stride = vision * per_device
    source = (offset // per_device * stride + owner * per_device + offset % per_device).astype(jnp.int32)
    slots = jnp.arange(stride * group_size, dtype=jnp.int32)
    within = slots % stride
    slot_owner = within // per_device
    slot_offset = (slots // stride * per_device + within % per_device).astype(jnp.int32)
    owner_start = lax.optimization_barrier(jnp.sum(chosen * block_starts[:, None], axis=0)).astype(jnp.int32)
    matched = (slot_owner[:, None] == labels[None, :]).astype(jnp.int32)
    start_of = lax.optimization_barrier(jnp.sum(matched * owner_start[None, :], axis=1)).astype(jnp.int32)
    count_of = lax.optimization_barrier(jnp.sum(matched * counts[None, :], axis=1)).astype(jnp.int32)
    live = slot_offset < count_of
    target = jnp.where(live, start_of + slot_offset, 0).astype(jnp.int32)
    return (source, target, live)

def gelu_parts(pre):
    normal_cdf = 0.5 * (1.0 + jax.scipy.special.erf(pre * 0.7071067811865476))
    density = jnp.exp(-0.5 * pre * pre) * 0.3989422804014327
    return (pre * normal_cdf, normal_cdf + pre * density)

def apply_layer_norm(images, projector_norm_gain):
    values = images.astype(jnp.float32)
    mean_removed = values - lax.optimization_barrier(jnp.mean(values, axis=-1, keepdims=True))
    variance = lax.optimization_barrier(jnp.mean(mean_removed * mean_removed, axis=-1, keepdims=True))
    inverse_scale = lax.rsqrt(variance + 1e-05)
    standardized_input = mean_removed * inverse_scale
    return (standardized_input, inverse_scale, (standardized_input * projector_norm_gain).astype(jnp.bfloat16))

def norm_gradient_pass(gradient_tuple, standardized_input, inverse_scale, projector_norm_gain):
    gain_scaled = gradient_tuple * projector_norm_gain
    return inverse_scale * (gain_scaled - lax.optimization_barrier(jnp.mean(gain_scaled, axis=-1, keepdims=True)) - standardized_input * lax.optimization_barrier(jnp.mean(gain_scaled * standardized_input, axis=-1, keepdims=True)))

def product(left, right):
    return jnp.dot(left, right, preferred_element_type=jnp.float32)

def rounded(value):
    return lax.optimization_barrier(value.astype(jnp.bfloat16)).astype(jnp.float32)

def reference(images, counts, block_order, projector_norm_gain, proj_first, proj_bias, proj_second, gate_weight, up_weight, down_weight, cotangent):
    source, target, live = row_tables(counts, block_order, ROWS, CAP, 1)
    standardized_input, inverse_scale, norm_output = apply_layer_norm(images, projector_norm_gain)
    packed = jnp.take(norm_output, source, axis=0)
    pre = product(packed, proj_first) + proj_bias
    activated, slope = gelu_parts(pre)
    hidden_proj = activated.astype(jnp.bfloat16)
    inputs = product(hidden_proj, proj_second).astype(jnp.bfloat16)
    width = D // N_VIS
    gate_sum = jnp.zeros((ROWS, FF), jnp.float32)
    up_sum = jnp.zeros((ROWS, FF), jnp.float32)
    hidden_grad = jnp.zeros((ROWS, FF), jnp.float32)
    for section in range(N_VIS):
        lower = section * width
        upper = lower + width
        gate_sum = gate_sum + rounded(product(inputs[:, lower:upper], gate_weight[lower:upper]))
        up_sum = up_sum + rounded(product(inputs[:, lower:upper], up_weight[lower:upper]))
        hidden_grad = hidden_grad + rounded(product(cotangent[:, lower:upper], down_weight[:, lower:upper].T))
    gate_sigmoid = jax.nn.sigmoid(gate_sum)
    hidden = (gate_sum * gate_sigmoid * up_sum).astype(jnp.bfloat16)
    block_out = (inputs.astype(jnp.float32) + product(hidden, down_weight)).astype(jnp.bfloat16)
    gate_grad = (hidden_grad * up_sum * gate_sigmoid * (1.0 + gate_sum * (1.0 - gate_sigmoid))).astype(jnp.bfloat16)
    up_grad = (hidden_grad * gate_sum * gate_sigmoid).astype(jnp.bfloat16)
    input_grad = (cotangent.astype(jnp.float32) + product(gate_grad, gate_weight.T) + product(up_grad, up_weight.T)).astype(jnp.bfloat16)
    second_grad = product(hidden_proj.T, input_grad)
    pre_grad = product(input_grad, proj_second.T)
    act_grad = (pre_grad * slope).astype(jnp.bfloat16)
    first_grad = product(packed.T, act_grad)
    normed_grad = product(act_grad, proj_first.T)
    slot_gradient = jnp.where(live[:, None], jnp.take(normed_grad, target, axis=0), jnp.zeros((), jnp.float32))
    image_slot_gradients = norm_gradient_pass(slot_gradient, standardized_input, inverse_scale, projector_norm_gain)
    return (block_out, image_slot_gradients, first_grad, second_grad)
```

```python
import functools

import jax
import jax.numpy as jnp
from jax import lax
from jax.experimental import pallas as pl
from jax.experimental.pallas import tpu as pltpu
from jax.sharding import PartitionSpec as P


def row_tables(counts, block_order, total_rows, per_device, group_size):
    vision = counts.shape[0]
    labels = jnp.arange(vision, dtype=jnp.int32)
    chosen = (block_order[:, None] == labels[None, :]).astype(jnp.int32)
    ordered = jnp.sum(chosen * counts[None, :], axis=1)
    block_ends = jnp.cumsum(ordered)
    block_starts = block_ends - ordered
    language = jnp.arange(total_rows, dtype=jnp.int32)
    block_of = jnp.sum((block_ends[None, :] <= language[:, None]).astype(jnp.int32), axis=1)
    picked = (block_of[:, None] == labels[None, :]).astype(jnp.int32)
    owner = jnp.sum(picked * block_order[None, :], axis=1)
    offset = language - jnp.sum(picked * block_starts[None, :], axis=1)
    stride = vision * per_device
    source = offset // per_device * stride + owner * per_device + offset % per_device
    slots = jnp.arange(stride * group_size, dtype=jnp.int32)
    within = slots % stride
    slot_owner = within // per_device
    slot_offset = slots // stride * per_device + within % per_device
    owner_start = jnp.sum(chosen * block_starts[:, None], axis=0)
    matched = (slot_owner[:, None] == labels[None, :]).astype(jnp.int32)
    start_of = jnp.sum(matched * owner_start[None, :], axis=1)
    count_of = jnp.sum(matched * counts[None, :], axis=1)
    live = slot_offset < count_of
    target = jnp.where(live, start_of + slot_offset, 0)
    return (source, target, live)


def gelu_parts(pre):
    normal_cdf = 0.5 * (1.0 + jax.scipy.special.erf(pre * 0.7071067811865476))
    density = jnp.exp(-0.5 * pre * pre) * 0.3989422804014327
    return (pre * normal_cdf, normal_cdf + pre * density)


def apply_layer_norm(images, projector_norm_gain):
    values = images.astype(jnp.float32)
    mean_removed = values - jnp.mean(values, axis=-1, keepdims=True)
    variance = jnp.mean(mean_removed * mean_removed, axis=-1, keepdims=True)
    inverse_scale = lax.rsqrt(variance + 1e-05)
    standardized_input = mean_removed * inverse_scale
    return (
        standardized_input,
        inverse_scale,
        (standardized_input * projector_norm_gain).astype(jnp.bfloat16),
    )


def norm_gradient_pass(gradient_tuple, standardized_input, inverse_scale, projector_norm_gain):
    gain_scaled = gradient_tuple * projector_norm_gain
    return inverse_scale * (
        gain_scaled
        - jnp.mean(gain_scaled, axis=-1, keepdims=True)
        - standardized_input * jnp.mean(gain_scaled * standardized_input, axis=-1, keepdims=True)
    )


def product(left, right):
    return jnp.dot(left, right, preferred_element_type=jnp.float32)


def feed_grads(hidden_grad, gate_sum, up_sum, gate_sigmoid):
    gate_grad = (
        hidden_grad * up_sum * gate_sigmoid * (1.0 + gate_sum * (1.0 - gate_sigmoid))
    ).astype(jnp.bfloat16)
    up_grad = (hidden_grad * gate_sum * gate_sigmoid).astype(jnp.bfloat16)
    return (gate_grad, up_grad)


MESH = pl.DeviceIdType.MESH
BF = jnp.bfloat16
F32 = jnp.float32
ANY = pl.BlockSpec(memory_space=pl.ANY)
VM = pl.BlockSpec(memory_space=pltpu.VMEM)
TILES = 4


def dot_nt(left, right):
    return lax.dot_general(left, right, (((1,), (1,)), ((), ())), preferred_element_type=F32)


def entry_barrier(n, me, coords):
    barrier = pltpu.get_barrier_semaphore()

    def signal(k, carry):
        pl.semaphore_signal(
            barrier, inc=1, device_id=coords(lax.rem(me + k, n)), device_id_type=MESH
        )
        return carry

    lax.fori_loop(1, n, signal, 0)
    return barrier


def spread(src_of, dst, n, me, coords, send_sem, recv_sem):
    def body(k, carry):
        p = lax.rem(me + k, n)
        pltpu.make_async_remote_copy(
            src_ref=src_of(p),
            dst_ref=dst.at[me],
            send_sem=send_sem,
            recv_sem=recv_sem,
            device_id=coords(p),
            device_id_type=MESH,
        ).start()
        return carry

    lax.fori_loop(1, n, body, 0)


def wait_for(buf, n, sem):
    view = buf.at[pl.ds(0, n - 1)]
    pltpu.make_async_copy(view, view, sem).wait()


def flat_coords(sizes, p):
    n_vis, _, n_col = sizes
    return (p % n_vis, p // n_vis // n_col, p // n_vis % n_col)


def my_place(sizes):
    n_vis, _, n_col = sizes
    vis, row, col = lax.axis_index("vis"), lax.axis_index("row"), lax.axis_index("col")
    return vis, row, col, (row * n_col + col) * n_vis + vis


def gather_kernel(sizes, blocks, cot, rows_out, cot_out, sems):
    n_vis, n_row, n_col = sizes
    group = n_row * n_col
    n_dev = n_vis * group
    vis, row, col, me = my_place(sizes)
    pos = row * n_col + col
    barrier = entry_barrier(n_dev, me, lambda p: flat_coords(sizes, p))
    pl.semaphore_wait(barrier, n_dev - 1)
    spread(
        lambda p: blocks.at[lax.rem(p, n_vis)], rows_out, n_dev, me,
        lambda p: flat_coords(sizes, p), sems.at[0], sems.at[1],
    )
    spread(
        lambda p: cot, cot_out, group, pos,
        lambda p: (vis, p // n_col, p % n_col), sems.at[2], sems.at[3],
    )
    rows_out[me] = blocks[vis]
    cot_out[pos] = cot[...]
    wait_for(rows_out, n_dev, sems.at[1])
    wait_for(cot_out, group, sems.at[3])
    wait_for(rows_out, n_dev, sems.at[0])
    wait_for(cot_out, group, sems.at[2])


def return_kernel(sizes, slabs, recv, sems):
    n_vis, n_row, n_col = sizes
    n_dev = n_vis * n_row * n_col
    _, _, _, me = my_place(sizes)
    barrier = entry_barrier(n_dev, me, lambda p: flat_coords(sizes, p))
    pl.semaphore_wait(barrier, n_dev - 1)
    spread(
        lambda p: slabs.at[p], recv, n_dev, me,
        lambda p: flat_coords(sizes, p), sems.at[0], sems.at[1],
    )
    recv[me] = slabs[me]
    wait_for(recv, n_dev, sems.at[1])
    wait_for(recv, n_dev, sems.at[0])


def middle_kernel(
    sizes, packed, upstream, bias, wf_hbm, ws_hbm, wg_hbm, wu_hbm, wd_hbm,
    block_out, act_out, hid_out, ig_out,
    wf, ws, wg, wu, wd,
    b_part, b_recv, b_all, h_part, h_recv, h_all, c_part, c_recv, c_all,
    d_part, d_recv, d_all, e_part, e_recv, e_all, o_part, o_recv, f_part, f_recv, f_all,
    slope, inputs, acc, hidden, wsem, sems,
):
    n_vis, n_row, n_col = sizes
    group = n_row * n_col
    vis, row, col, _ = my_place(sizes)
    pos = row * n_col + col
    rows = packed.shape[0]
    vr, gr = rows // n_vis, rows // group
    ffl = wg.shape[1]
    tw = ffl // TILES

    def in_vis(p):
        return (p, row, col)

    def in_group(p):
        return (vis, p // n_col, p % n_col)

    loads = {}
    for i, (name, src, dst) in enumerate(
        (("wf", wf_hbm, wf), ("wd", wd_hbm, wd), ("ws", ws_hbm, ws), ("wg", wg_hbm, wg), ("wu", wu_hbm, wu))
    ):
        loads[name] = pltpu.make_async_copy(src, dst, wsem.at[i])
        loads[name].start()
    barrier = entry_barrier(n_vis, vis, in_vis)
    entry_barrier(group, pos, in_group)

    used = []

    def start(idx, src_of, dst, n, me, coords):
        spread(src_of, dst, n, me, coords, sems.at[2 * idx], sems.at[2 * idx + 1])
        used.append((idx, dst, n))

    def arrive(idx, dst, n):
        wait_for(dst, n, sems.at[2 * idx + 1])

    def fill(part, value, n, chunk):
        for i in range(n):
            part[i] = value[i * chunk:(i + 1) * chunk].astype(BF)

    def total(recv, part, n, me):
        recv[me] = part[me]
        result = recv[0].astype(F32)
        for i in range(1, n):
            result = result + recv[i].astype(F32)
        return result

    def whole(buf, n):
        return jnp.concatenate([buf[i].astype(F32) for i in range(n)], axis=0)

    loads["wf"].wait()
    fill(b_part, jnp.dot(packed[...], wf[...], preferred_element_type=F32), n_vis, vr)
    pl.semaphore_wait(barrier, n_vis - 1 + group - 1)
    start(0, lambda p: b_part.at[p], b_recv, n_vis, vis, in_vis)

    loads["wd"].wait()
    for t in range(TILES):
        cols = slice(t * tw, (t + 1) * tw)
        value = dot_nt(upstream[...], wd[cols, :])
        for i in range(n_vis):
            h_part[i, :, cols] = value[i * vr:(i + 1) * vr].astype(BF)

    arrive(0, b_recv, n_vis)
    b_all[vis] = total(b_recv, b_part, n_vis, vis).astype(BF)
    start(1, lambda p: b_all.at[vis], b_all, n_vis, vis, in_vis)
    start(2, lambda p: h_part.at[p], h_recv, n_vis, vis, in_vis)
    arrive(1, b_all, n_vis)
    pre = whole(b_all, n_vis) + bias[...]
    activated, slope_value = gelu_parts(pre)
    slope[...] = slope_value
    hid_out[...] = activated.astype(BF)

    loads["ws"].wait()
    fill(c_part, jnp.dot(hid_out[...], ws[...], preferred_element_type=F32), group, gr)
    start(3, lambda p: c_part.at[p], c_recv, group, pos, in_group)
    arrive(2, h_recv, n_vis)
    h_all[vis] = total(h_recv, h_part, n_vis, vis).astype(BF)
    start(4, lambda p: h_all.at[vis], h_all, n_vis, vis, in_vis)
    arrive(3, c_recv, group)
    c_all[pos] = total(c_recv, c_part, group, pos).astype(BF)
    start(5, lambda p: c_all.at[pos], c_all, group, pos, in_group)
    arrive(5, c_all, group)
    inputs[...] = whole(c_all, group).astype(BF)

    loads["wg"].wait()
    loads["wu"].wait()
    arrive(4, h_all, n_vis)
    for t in range(TILES):
        cols = slice(t * tw, (t + 1) * tw)
        for half, weight in enumerate((wg, wu)):
            value = jnp.dot(inputs[...], weight[:, cols], preferred_element_type=F32)
            for i in range(n_vis):
                d_part[t, i, :, half * tw:(half + 1) * tw] = value[i * vr:(i + 1) * vr].astype(BF)
        start(6 + t, lambda p, t=t: d_part.at[t, p], d_recv.at[t], n_vis, vis, in_vis)
    for t in range(TILES):
        arrive(6 + t, d_recv.at[t], n_vis)
        d_all[t, vis] = total(d_recv.at[t], d_part.at[t], n_vis, vis).astype(BF)
        start(6 + TILES + t, lambda p, t=t: d_all.at[t, vis], d_all.at[t], n_vis, vis, in_vis)
    for t in range(TILES):
        cols = slice(t * tw, (t + 1) * tw)
        arrive(6 + TILES + t, d_all.at[t], n_vis)
        both = whole(d_all.at[t], n_vis)
        gate_sum, up_sum = both[:, :tw], both[:, tw:]
        hidden_grad = jnp.concatenate([h_all[i, :, cols].astype(F32) for i in range(n_vis)], axis=0)
        gate_sigmoid = jax.nn.sigmoid(gate_sum)
        hidden[:, cols] = (gate_sum * gate_sigmoid * up_sum).astype(BF)
        gate_grad, up_grad = feed_grads(hidden_grad, gate_sum, up_sum, gate_sigmoid)
        value = dot_nt(gate_grad, wg[:, cols]) + dot_nt(up_grad, wu[:, cols])
        if t == 0:
            acc[...] = value
        else:
            acc[...] += value
    base = 6 + 2 * TILES
    fill(e_part, acc[...], group, gr)
    start(base, lambda p: e_part.at[p], e_recv, group, pos, in_group)

    fill(o_part, jnp.dot(hidden[...], wd[...], preferred_element_type=F32), group, gr)
    arrive(base, e_recv, group)
    mine = pl.ds(pl.multiple_of(pos * gr, gr), gr)
    e_all[pos] = (total(e_recv, e_part, group, pos) + upstream[mine, :].astype(F32)).astype(BF)
    start(base + 1, lambda p: e_all.at[pos], e_all, group, pos, in_group)
    start(base + 2, lambda p: o_part.at[p], o_recv, group, pos, in_group)
    arrive(base + 1, e_all, group)
    ig_out[...] = whole(e_all, group).astype(BF)
    fill(f_part, dot_nt(ig_out[...], ws[...]), n_vis, vr)
    start(base + 3, lambda p: f_part.at[p], f_recv, n_vis, vis, in_vis)
    arrive(base + 3, f_recv, n_vis)
    f_all[vis] = total(f_recv, f_part, n_vis, vis).astype(BF)
    start(base + 4, lambda p: f_all.at[vis], f_all, n_vis, vis, in_vis)
    arrive(base + 2, o_recv, group)
    block_out[...] = (c_all[pos].astype(F32) + total(o_recv, o_part, group, pos)).astype(BF)
    arrive(base + 4, f_all, n_vis)
    act_out[...] = (whole(f_all, n_vis) * slope[...]).astype(BF)
    for idx, dst, n in used:
        wait_for(dst, n, sems.at[2 * idx])


def slabs_of(n, *shape):
    return [pltpu.VMEM((n,) + shape, BF)] * 3


def on_device(
    sizes,
    images,
    counts,
    block_order,
    projector_norm_gain,
    proj_first,
    proj_bias,
    proj_second,
    gate_weight,
    up_weight,
    down_weight,
    cotangent,
):
    n_vis, n_row, n_col = sizes
    group_size = n_row * n_col
    n_dev = n_vis * group_size
    per_device = images.shape[0]
    local_rows = cotangent.shape[0]
    rows = local_rows * group_size
    vf, pl_units = proj_first.shape
    dl, ffl = gate_weight.shape
    source, target, live = row_tables(counts, block_order, rows, per_device, group_size)
    standardized_input, inverse_scale, norm_output = apply_layer_norm(images, projector_norm_gain)
    blocks = jnp.swapaxes(norm_output.reshape(per_device, n_vis, vf), 0, 1)
    gathered, upstream = pl.pallas_call(
        functools.partial(gather_kernel, sizes),
        out_shape=(
            jax.ShapeDtypeStruct((n_dev, per_device, vf), BF),
            jax.ShapeDtypeStruct((group_size, local_rows, dl), BF),
        ),
        in_specs=[VM, VM],
        out_specs=(VM, VM),
        scratch_shapes=[pltpu.SemaphoreType.DMA((4,))],
        compiler_params=pltpu.CompilerParams(collective_id=0, has_side_effects=True),
    )(blocks, cotangent)
    upstream = upstream.reshape(rows, dl)
    packed = jnp.take(gathered.reshape(n_dev * per_device, vf), source, axis=0)
    vr = rows // n_vis
    n_sems = 2 * (6 + 2 * TILES + 5)
    block_out, act_grad, hidden_proj, input_grad = pl.pallas_call(
        functools.partial(middle_kernel, sizes),
        out_shape=(
            jax.ShapeDtypeStruct((local_rows, dl), BF),
            jax.ShapeDtypeStruct((rows, pl_units), BF),
            jax.ShapeDtypeStruct((rows, pl_units), BF),
            jax.ShapeDtypeStruct((rows, dl), BF),
        ),
        in_specs=[VM, VM, VM, ANY, ANY, ANY, ANY, ANY],
        out_specs=(VM, VM, VM, VM),
        scratch_shapes=[
            pltpu.VMEM(proj_first.shape, BF),
            pltpu.VMEM(proj_second.shape, BF),
            pltpu.VMEM(gate_weight.shape, BF),
            pltpu.VMEM(up_weight.shape, BF),
            pltpu.VMEM(down_weight.shape, BF),
            *slabs_of(n_vis, vr, pl_units),
            *slabs_of(n_vis, vr, ffl),
            *slabs_of(group_size, local_rows, dl),
            *slabs_of(TILES, n_vis, vr, 2 * ffl // TILES),
            *slabs_of(group_size, local_rows, dl),
            *slabs_of(group_size, local_rows, dl)[:2],
            *slabs_of(n_vis, vr, pl_units),
            pltpu.VMEM((rows, pl_units), F32),
            pltpu.VMEM((rows, dl), BF),
            pltpu.VMEM((rows, dl), F32),
            pltpu.VMEM((rows, ffl), BF),
            pltpu.SemaphoreType.DMA((5,)),
            pltpu.SemaphoreType.DMA((n_sems,)),
        ],
        compiler_params=pltpu.CompilerParams(
            collective_id=1, has_side_effects=True, vmem_limit_bytes=48 << 20
        ),
    )(
        packed, upstream, proj_bias[None, :], proj_first, proj_second,
        gate_weight, up_weight, down_weight,
    )
    slot_act = jnp.where(
        live[:, None], jnp.take(act_grad, target, axis=0), jnp.zeros((), BF)
    )
    slot_part = dot_nt(slot_act, proj_first).astype(BF)
    returned = pl.pallas_call(
        functools.partial(return_kernel, sizes),
        out_shape=jax.ShapeDtypeStruct((n_dev, per_device, vf), BF),
        in_specs=[VM],
        out_specs=VM,
        scratch_shapes=[pltpu.SemaphoreType.DMA((2,))],
        compiler_params=pltpu.CompilerParams(collective_id=2, has_side_effects=True),
    )(slot_part.reshape(n_dev, per_device, vf))
    returned = jnp.sum(returned.reshape(group_size, n_vis, per_device, vf).astype(F32), axis=0)
    image_slot_gradients = norm_gradient_pass(
        jnp.swapaxes(returned, 0, 1).reshape(per_device, n_vis * vf),
        standardized_input, inverse_scale, projector_norm_gain,
    )
    second_grad = product(hidden_proj.T, input_grad)
    first_grad = product(packed.T, act_grad)
    return (block_out, image_slot_gradients, first_grad, second_grad)


def solution(mesh):
    in_specs = (
        P(("vis", "row", "col"), None),
        P(),
        P(),
        P(),
        P("vis", ("row", "col")),
        P(("row", "col")),
        P(("row", "col"), "vis"),
        P("vis", ("row", "col")),
        P("vis", ("row", "col")),
        P(("row", "col"), "vis"),
        P(("row", "col"), "vis"),
    )
    out_specs = (
        P(("row", "col"), "vis"),
        P(("vis", "row", "col"), None),
        P("vis", ("row", "col")),
        P(("row", "col"), "vis"),
    )
    sizes = (mesh.shape["vis"], mesh.shape["row"], mesh.shape["col"])
    return jax.shard_map(
        functools.partial(on_device, sizes), mesh=mesh, in_specs=in_specs, out_specs=out_specs, check_vma=False
    )
```

```python
import functools

import jax
import jax.numpy as jnp
from jax import lax
from jax.experimental import pallas as pl
from jax.experimental.pallas import tpu as pltpu
from jax.sharding import PartitionSpec as P


def gelu_parts(pre):
    normal_cdf = 0.5 * (1.0 + jax.scipy.special.erf(pre * 0.7071067811865476))
    density = jnp.exp(-0.5 * pre * pre) * 0.3989422804014327
    return (pre * normal_cdf, normal_cdf + pre * density)


def norm_gradient_pass(gradient_tuple, standardized_input, inverse_scale, projector_norm_gain):
    gain_scaled = gradient_tuple * projector_norm_gain
    return inverse_scale * (
        gain_scaled
        - jnp.mean(gain_scaled, axis=-1, keepdims=True)
        - standardized_input * jnp.mean(gain_scaled * standardized_input, axis=-1, keepdims=True)
    )


def product(left, right):
    return jnp.dot(left, right, preferred_element_type=jnp.float32)


def feed_grads(hidden_grad, gate_sum, up_sum, gate_sigmoid):
    gate_grad = (
        hidden_grad * up_sum * gate_sigmoid * (1.0 + gate_sum * (1.0 - gate_sigmoid))
    ).astype(jnp.bfloat16)
    up_grad = (hidden_grad * gate_sum * gate_sigmoid).astype(jnp.bfloat16)
    return (gate_grad, up_grad)


MESH = pl.DeviceIdType.MESH
BF = jnp.bfloat16
F32 = jnp.float32
ANY = pl.BlockSpec(memory_space=pl.ANY)
VM = pl.BlockSpec(memory_space=pltpu.VMEM)
TILES = 4


def dot_nt(left, right):
    return lax.dot_general(left, right, (((1,), (1,)), ((), ())), preferred_element_type=F32)


def entry_barrier(n, me, coords):
    barrier = pltpu.get_barrier_semaphore()

    def signal(k, carry):
        pl.semaphore_signal(
            barrier, inc=1, device_id=coords(lax.rem(me + k, n)), device_id_type=MESH
        )
        return carry

    lax.fori_loop(1, n, signal, 0)
    return barrier


def spread(src_of, dst, n, me, coords, send_sem, recv_sem):
    def body(k, carry):
        p = lax.rem(me + k, n)
        pltpu.make_async_remote_copy(
            src_ref=src_of(p),
            dst_ref=dst.at[me],
            send_sem=send_sem,
            recv_sem=recv_sem,
            device_id=coords(p),
            device_id_type=MESH,
        ).start()
        return carry

    lax.fori_loop(1, n, body, 0)


def wait_for(view, sem):
    pltpu.make_async_copy(view, view, sem).wait()


def flat_coords(sizes, p):
    n_vis, _, n_col = sizes
    return (p % n_vis, p // n_vis // n_col, p // n_vis % n_col)


def my_place(sizes):
    n_vis, _, n_col = sizes
    vis, row, col = lax.axis_index("vis"), lax.axis_index("row"), lax.axis_index("col")
    return vis, row, col, (row * n_col + col) * n_vis + vis


def row_places(counts, order, n_vis, per, shape, axis):
    slots = lax.broadcasted_iota(jnp.int32, shape, axis)
    owner = slots // per % n_vis
    offset = slots // (n_vis * per) * per + slots % per
    start_of = jnp.zeros(shape, jnp.int32)
    count_of = jnp.zeros(shape, jnp.int32)
    begin = jnp.int32(0)
    for b in range(n_vis):
        device = order[b]
        live_rows = counts[device]
        start_of = jnp.where(owner == device, begin, start_of)
        count_of = jnp.where(owner == device, live_rows, count_of)
        begin = begin + live_rows
    return jnp.where(offset < count_of, start_of + offset, -1)


def chain_kernel(
    sizes, counts, order, images, gain, cot, bias, wf_hbm, ws_hbm, wg_hbm, wu_hbm, wd_hbm,
    block_out, slot_out, packed_out, act_out, hid_out, ig_out,
    wf, ws, wg, wu, wd,
    blocks, rows_all, cot_all, upstream, slabs, slabs_recv,
    b_part, b_pair, b_ring, b_all, h_part, h_pair, h_ring, h_all,
    d_part, d_pair, d_ring, d_all, f_part, f_pair, f_ring, f_all,
    c_part, c_recv, c_all, e_part, e_recv, e_all, o_part, o_recv,
    slope, inputs, acc, hidden, wsem, sems,
):
    n_vis, n_row, n_col = sizes
    group = n_row * n_col
    n_dev = n_vis * group
    vis, row, col, me = my_place(sizes)
    pos = row * n_col + col
    core, ring_at, n_ring = lax.rem(vis, 2), vis // 2, n_vis // 2
    per, vf = blocks.shape[1:]
    rows, dl = upstream.shape
    gr, hr = rows // group, rows // 2
    ffl = wg.shape[1]
    tw = ffl // TILES

    def everyone(p):
        return flat_coords(sizes, p)

    def in_ring(p):
        return (2 * p + core, row, col)

    def in_group(p):
        return (vis, p // n_col, p % n_col)

    loads = {}
    for i, (name, src, dst) in enumerate(
        (("wd", wd_hbm, wd), ("wf", wf_hbm, wf), ("ws", ws_hbm, ws), ("wg", wg_hbm, wg), ("wu", wu_hbm, wu))
    ):
        loads[name] = pltpu.make_async_copy(src, dst, wsem.at[i])
        loads[name].start()
    barrier = entry_barrier(n_dev, me, everyone)

    sent = []

    def pair_of_sems(view):
        idx = 2 * len(sent)
        sent.append((view, sems.at[idx]))
        return sems.at[idx], sems.at[idx + 1]

    def start(src_of, dst, n, at, coords):
        view = dst.at[pl.ds(0, n - 1)]
        send_sem, recv_sem = pair_of_sems(view)
        spread(src_of, dst, n, at, coords, send_sem, recv_sem)
        return lambda: wait_for(view, recv_sem)

    def to_partner(src, dst):
        send_sem, recv_sem = pair_of_sems(dst)
        pltpu.make_async_remote_copy(
            src_ref=src, dst_ref=dst, send_sem=send_sem, recv_sem=recv_sem,
            device_id=(2 * ring_at + 1 - core, row, col), device_id_type=MESH,
        ).start()
        return lambda: wait_for(dst, recv_sem)

    def vis_begin(part, pair):
        return to_partner(part.at[1 - core], pair)

    def vis_middle(arrived, part, pair, ring):
        arrived()
        ring[ring_at] = (part[core].astype(F32) + pair[...].astype(F32)).astype(BF)
        return start(lambda p: ring.at[ring_at], ring, n_ring, ring_at, in_ring)

    def vis_finish(arrived, ring, result):
        arrived()
        value = ring[0].astype(F32)
        for i in range(1, n_ring):
            value = value + ring[i].astype(F32)
        result[core] = value.astype(BF)
        return to_partner(result.at[core], result.at[core])

    def fill(part, value, n, chunk):
        for i in range(n):
            part[i] = value[i * chunk:(i + 1) * chunk].astype(BF)

    def total(recv, part, n, at):
        recv[at] = part[at]
        result = recv[0].astype(F32)
        for i in range(1, n):
            result = result + recv[i].astype(F32)
        return result

    def whole(buf, n):
        return jnp.concatenate([buf[i].astype(F32) for i in range(n)], axis=0)

    values = images[...].astype(F32)
    centred = values - jnp.mean(values, axis=-1, keepdims=True)
    inverse_scale = lax.rsqrt(jnp.mean(centred * centred, axis=-1, keepdims=True) + 1e-05)
    normed = centred * inverse_scale * gain[...]
    for i in range(n_vis):
        blocks[i] = normed[:, i * vf:(i + 1) * vf].astype(BF)
    pl.semaphore_wait(barrier, n_dev - 1)
    cot_done = start(lambda p: cot, cot_all, group, pos, in_group)
    rows_done = start(lambda p: blocks.at[lax.rem(p, n_vis)], rows_all, n_dev, me, everyone)
    cot_all[pos] = cot[...]
    rows_all[me] = blocks[vis]

    cot_done()
    upstream[...] = whole(cot_all, group).astype(BF)
    loads["wd"].wait()
    for t in range(TILES):
        cols = slice(t * tw, (t + 1) * tw)
        value = dot_nt(upstream[...], wd[cols, :])
        for i in range(2):
            h_part[i, :, cols] = value[i * hr:(i + 1) * hr].astype(BF)
    h_done = vis_begin(h_part, h_pair)
    n_slots = n_dev * per
    place = row_places(counts, order, n_vis, per, (rows, n_slots), 1)
    pick = jnp.where(place == lax.broadcasted_iota(jnp.int32, (rows, n_slots), 0), 1.0, 0.0).astype(BF)

    loads["wf"].wait()
    rows_done()
    packed_out[...] = jnp.dot(
        pick, rows_all[...].reshape(n_slots, vf), preferred_element_type=F32
    ).astype(BF)
    fill(b_part, jnp.dot(packed_out[...], wf[...], preferred_element_type=F32), 2, hr)
    b_done = vis_begin(b_part, b_pair)
    b_done = vis_middle(b_done, b_part, b_pair, b_ring)
    h_done = vis_middle(h_done, h_part, h_pair, h_ring)
    b_done = vis_finish(b_done, b_ring, b_all)
    b_done()
    pre = whole(b_all, 2) + bias[...]
    activated, slope_value = gelu_parts(pre)
    slope[...] = slope_value
    hid_out[...] = activated.astype(BF)

    loads["ws"].wait()
    fill(c_part, jnp.dot(hid_out[...], ws[...], preferred_element_type=F32), group, gr)
    c_done = start(lambda p: c_part.at[p], c_recv, group, pos, in_group)
    h_done = vis_finish(h_done, h_ring, h_all)
    c_done()
    c_all[pos] = total(c_recv, c_part, group, pos).astype(BF)
    c_done = start(lambda p: c_all.at[pos], c_all, group, pos, in_group)
    loads["wg"].wait()
    loads["wu"].wait()
    h_done()
    c_done()
    inputs[...] = whole(c_all, group).astype(BF)

    d_done = [None] * TILES
    for t in range(TILES):
        cols = slice(t * tw, (t + 1) * tw)
        for half, weight in enumerate((wg, wu)):
            value = jnp.dot(inputs[...], weight[:, cols], preferred_element_type=F32)
            for i in range(2):
                d_part[t, i, :, half * tw:(half + 1) * tw] = value[i * hr:(i + 1) * hr].astype(BF)
        d_done[t] = vis_begin(d_part.at[t], d_pair.at[t])
        if t > 0:
            d_done[t - 1] = vis_middle(d_done[t - 1], d_part.at[t - 1], d_pair.at[t - 1], d_ring.at[t - 1])
    d_done[-1] = vis_middle(d_done[-1], d_part.at[TILES - 1], d_pair.at[TILES - 1], d_ring.at[TILES - 1])
    d_done[0] = vis_finish(d_done[0], d_ring.at[0], d_all.at[0])
    for t in range(TILES):
        if t + 1 < TILES:
            d_done[t + 1] = vis_finish(d_done[t + 1], d_ring.at[t + 1], d_all.at[t + 1])
        d_done[t]()
        cols = slice(t * tw, (t + 1) * tw)
        both = whole(d_all.at[t], 2)
        gate_sum, up_sum = both[:, :tw], both[:, tw:]
        hidden_grad = jnp.concatenate([h_all[i, :, cols].astype(F32) for i in range(2)], axis=0)
        gate_sigmoid = jax.nn.sigmoid(gate_sum)
        hidden[:, cols] = (gate_sum * gate_sigmoid * up_sum).astype(BF)
        gate_grad, up_grad = feed_grads(hidden_grad, gate_sum, up_sum, gate_sigmoid)
        value = dot_nt(gate_grad, wg[:, cols]) + dot_nt(up_grad, wu[:, cols])
        if t == 0:
            acc[...] = value
        else:
            acc[...] += value
    fill(e_part, acc[...], group, gr)
    e_done = start(lambda p: e_part.at[p], e_recv, group, pos, in_group)

    fill(o_part, jnp.dot(hidden[...], wd[...], preferred_element_type=F32), group, gr)
    e_done()
    e_all[pos] = (total(e_recv, e_part, group, pos) + cot[...].astype(F32)).astype(BF)
    e_done = start(lambda p: e_all.at[pos], e_all, group, pos, in_group)
    o_done = start(lambda p: o_part.at[p], o_recv, group, pos, in_group)
    place = row_places(counts, order, n_vis, per, (n_slots, rows), 0)
    put = jnp.where(place == lax.broadcasted_iota(jnp.int32, (n_slots, rows), 1), 1.0, 0.0).astype(BF)
    e_done()
    ig_out[...] = whole(e_all, group).astype(BF)
    fill(f_part, dot_nt(ig_out[...], ws[...]), 2, hr)
    f_done = vis_begin(f_part, f_pair)
    f_done = vis_middle(f_done, f_part, f_pair, f_ring)
    o_done()
    block_out[...] = (c_all[pos].astype(F32) + total(o_recv, o_part, group, pos)).astype(BF)
    f_done = vis_finish(f_done, f_ring, f_all)
    f_done()
    act_out[...] = (whole(f_all, 2) * slope[...]).astype(BF)

    slot_act = jnp.dot(put, act_out[...], preferred_element_type=F32).astype(BF)
    slabs[...] = dot_nt(slot_act, wf[...]).astype(BF).reshape(n_dev, per, vf)
    slabs_done = start(lambda p: slabs.at[p], slabs_recv, n_dev, me, everyone)
    slabs_recv[me] = slabs[me]
    slabs_done()
    pieces = []
    for i in range(n_vis):
        value = slabs_recv[i].astype(F32)
        for g in range(1, group):
            value = value + slabs_recv[g * n_vis + i].astype(F32)
        pieces.append(value)
    standardized_input = centred * inverse_scale
    slot_out[...] = norm_gradient_pass(
        jnp.concatenate(pieces, axis=1), standardized_input, inverse_scale, gain[...]
    )
    for view, sem in sent:
        wait_for(view, sem)


def vis_buffers(n_vis, lead, half_rows, width):
    return [
        pltpu.VMEM(lead + (2, half_rows, width), BF),
        pltpu.VMEM(lead + (half_rows, width), BF),
        pltpu.VMEM(lead + (n_vis // 2, half_rows, width), BF),
        pltpu.VMEM(lead + (2, half_rows, width), BF),
    ]


def on_device(
    sizes,
    images,
    counts,
    block_order,
    projector_norm_gain,
    proj_first,
    proj_bias,
    proj_second,
    gate_weight,
    up_weight,
    down_weight,
    cotangent,
):
    n_vis, n_row, n_col = sizes
    group_size = n_row * n_col
    n_dev = n_vis * group_size
    per_device = images.shape[0]
    local_rows = cotangent.shape[0]
    rows = local_rows * group_size
    vf, units = proj_first.shape
    dl, ffl = gate_weight.shape
    hr = rows // 2
    by_group = pltpu.VMEM((group_size, local_rows, dl), BF)
    by_device = pltpu.VMEM((n_dev, per_device, vf), BF)
    sm = pl.BlockSpec(memory_space=pltpu.SMEM)
    n_sends = 3 * (3 + TILES) + 5 + 3
    block_out, image_slot_gradients, packed, act_grad, hidden_proj, input_grad = pl.pallas_call(
        functools.partial(chain_kernel, sizes),
        out_shape=(
            jax.ShapeDtypeStruct((local_rows, dl), BF),
            jax.ShapeDtypeStruct(images.shape, F32),
            jax.ShapeDtypeStruct((rows, vf), BF),
            jax.ShapeDtypeStruct((rows, units), BF),
            jax.ShapeDtypeStruct((rows, units), BF),
            jax.ShapeDtypeStruct((rows, dl), BF),
        ),
        in_specs=[sm, sm, VM, VM, VM, VM, ANY, ANY, ANY, ANY, ANY],
        out_specs=(VM,) * 6,
        scratch_shapes=[
            pltpu.VMEM(proj_first.shape, BF),
            pltpu.VMEM(proj_second.shape, BF),
            pltpu.VMEM(gate_weight.shape, BF),
            pltpu.VMEM(up_weight.shape, BF),
            pltpu.VMEM(down_weight.shape, BF),
            pltpu.VMEM((n_vis, per_device, vf), BF),
            by_device,
            by_group,
            pltpu.VMEM((rows, dl), BF),
            by_device,
            by_device,
            *vis_buffers(n_vis, (), hr, units),
            *vis_buffers(n_vis, (), hr, ffl),
            *vis_buffers(n_vis, (TILES,), hr, 2 * ffl // TILES),
            *vis_buffers(n_vis, (), hr, units),
            *[by_group] * 8,
            pltpu.VMEM((rows, units), F32),
            pltpu.VMEM((rows, dl), BF),
            pltpu.VMEM((rows, dl), F32),
            pltpu.VMEM((rows, ffl), BF),
            pltpu.SemaphoreType.DMA((5,)),
            pltpu.SemaphoreType.DMA((2 * n_sends,)),
        ],
        compiler_params=pltpu.CompilerParams(
            collective_id=0, has_side_effects=True, vmem_limit_bytes=48 << 20
        ),
    )(
        counts, block_order, images, projector_norm_gain[None, :], cotangent,
        proj_bias[None, :], proj_first, proj_second, gate_weight, up_weight, down_weight,
    )
    second_grad = product(hidden_proj.T, input_grad)
    first_grad = product(packed.T, act_grad)
    return (block_out, image_slot_gradients, first_grad, second_grad)


def solution(mesh):
    in_specs = (
        P(("vis", "row", "col"), None),
        P(),
        P(),
        P(),
        P("vis", ("row", "col")),
        P(("row", "col")),
        P(("row", "col"), "vis"),
        P("vis", ("row", "col")),
        P("vis", ("row", "col")),
        P(("row", "col"), "vis"),
        P(("row", "col"), "vis"),
    )
    out_specs = (
        P(("row", "col"), "vis"),
        P(("vis", "row", "col"), None),
        P("vis", ("row", "col")),
        P(("row", "col"), "vis"),
    )
    sizes = (mesh.shape["vis"], mesh.shape["row"], mesh.shape["col"])
    return jax.shard_map(
        functools.partial(on_device, sizes), mesh=mesh, in_specs=in_specs, out_specs=out_specs, check_vma=False
    )
```

```python
import functools

import jax
import jax.numpy as jnp
from jax import lax
from jax.experimental import pallas as pl
from jax.experimental.pallas import tpu as pltpu
from jax.sharding import PartitionSpec as P


def gelu_parts(pre):
    normal_cdf = 0.5 * (1.0 + jax.scipy.special.erf(pre * 0.7071067811865476))
    density = jnp.exp(-0.5 * pre * pre) * 0.3989422804014327
    return (pre * normal_cdf, normal_cdf + pre * density)


def norm_gradient_pass(gradient_tuple, standardized_input, inverse_scale, projector_norm_gain):
    gain_scaled = gradient_tuple * projector_norm_gain
    return inverse_scale * (
        gain_scaled
        - jnp.mean(gain_scaled, axis=-1, keepdims=True)
        - standardized_input * jnp.mean(gain_scaled * standardized_input, axis=-1, keepdims=True)
    )


def product(left, right):
    return jnp.dot(left, right, preferred_element_type=jnp.float32)


def feed_grads(hidden_grad, gate_sum, up_sum, gate_sigmoid):
    gate_grad = (
        hidden_grad * up_sum * gate_sigmoid * (1.0 + gate_sum * (1.0 - gate_sigmoid))
    ).astype(jnp.bfloat16)
    up_grad = (hidden_grad * gate_sum * gate_sigmoid).astype(jnp.bfloat16)
    return (gate_grad, up_grad)


MESH = pl.DeviceIdType.MESH
BF = jnp.bfloat16
F32 = jnp.float32
ANY = pl.BlockSpec(memory_space=pl.ANY)
VM = pl.BlockSpec(memory_space=pltpu.VMEM)
TILES = 4


def dot_nt(left, right):
    return lax.dot_general(left, right, (((1,), (1,)), ((), ())), preferred_element_type=F32)


def entry_barrier(n, me, coords):
    barrier = pltpu.get_barrier_semaphore()

    def signal(k, carry):
        pl.semaphore_signal(
            barrier, inc=1, device_id=coords(lax.rem(me + k, n)), device_id_type=MESH
        )
        return carry

    lax.fori_loop(1, n, signal, 0)
    return barrier


def spread(src_of, dst, n, me, coords, send_sem, recv_sem, slab=None):
    def body(k, carry):
        p = lax.rem(me + k, n)
        pltpu.make_async_remote_copy(
            src_ref=src_of(p),
            dst_ref=dst.at[me if slab is None else slab],
            send_sem=send_sem,
            recv_sem=recv_sem,
            device_id=coords(p),
            device_id_type=MESH,
        ).start()
        return carry

    lax.fori_loop(1, n, body, 0)


def wait_for(view, sem):
    pltpu.make_async_copy(view, view, sem).wait()


def flat_coords(sizes, p):
    n_vis, _, n_col = sizes
    return (p % n_vis, p // n_vis // n_col, p // n_vis % n_col)


def my_place(sizes):
    n_vis, _, n_col = sizes
    vis, row, col = lax.axis_index("vis"), lax.axis_index("row"), lax.axis_index("col")
    return vis, row, col, (row * n_col + col) * n_vis + vis


def row_places(counts, order, n_vis, per, shape, axis):
    slots = lax.broadcasted_iota(jnp.int32, shape, axis)
    owner = slots // per % n_vis
    offset = slots // (n_vis * per) * per + slots % per
    start_of = jnp.zeros(shape, jnp.int32)
    count_of = jnp.zeros(shape, jnp.int32)
    begin = jnp.int32(0)
    for b in range(n_vis):
        device = order[b]
        live_rows = counts[device]
        start_of = jnp.where(owner == device, begin, start_of)
        count_of = jnp.where(owner == device, live_rows, count_of)
        begin = begin + live_rows
    return jnp.where(offset < count_of, start_of + offset, -1)


def chain_kernel(
    sizes, counts_hbm, order_hbm, images_hbm, gain_hbm, cot_hbm, bias_hbm,
    wf_hbm, ws_hbm, wg_hbm, wu_hbm, wd_hbm,
    block_out, slot_out, packed_out, act_out, hid_out, ig_out,
    counts, order, images, gain, cot, bias, wf, ws, wg, wu, wd,
    blocks, rows_all, cot_all, upstream, slabs, across, column_sums, returned,
    b_part, b_pair, b_ring, b_all, h_part, h_pair, h_ring, h_all,
    d_part, d_pair, d_ring, d_all, f_part, f_pair, f_ring, f_all,
    c_part, c_recv, c_all, e_part, e_recv, e_all, o_part, o_recv,
    slope, inputs, acc, hidden, wsem, gather_sems, return_sems, sems,
):
    n_vis, n_row, n_col = sizes
    group = n_row * n_col
    n_dev = n_vis * group
    vis, row, col, me = my_place(sizes)
    pos = row * n_col + col
    core, ring_at, n_ring = lax.rem(vis, 2), vis // 2, n_vis // 2
    per, vf = blocks.shape[1:]
    rows, dl = upstream.shape
    gr, hr = rows // group, rows // 2
    ffl = wg.shape[1]
    tw = ffl // TILES

    def everyone(p):
        return flat_coords(sizes, p)

    def in_ring(p):
        return (2 * p + core, row, col)

    def in_column(p):
        return (lax.rem(p, n_vis), p // n_vis, col)

    def in_group(p):
        return (vis, p // n_col, p % n_col)

    loads = {}
    for i, (name, src, dst) in enumerate(
        (
            ("images", images_hbm, images), ("gain", gain_hbm, gain), ("cot", cot_hbm, cot),
            ("bias", bias_hbm, bias), ("counts", counts_hbm, counts), ("order", order_hbm, order),
            ("wd", wd_hbm, wd), ("wf", wf_hbm, wf), ("ws", ws_hbm, ws), ("wg", wg_hbm, wg), ("wu", wu_hbm, wu),
        )
    ):
        loads[name] = pltpu.make_async_copy(src, dst, wsem.at[i])
        loads[name].start()
    barrier = entry_barrier(n_dev, me, everyone)

    sent = []

    def pair_of_sems(view):
        idx = 2 * len(sent)
        sent.append((view, sems.at[idx]))
        return sems.at[idx], sems.at[idx + 1]

    def start(src_of, dst, n, at, coords):
        view = dst.at[pl.ds(0, n - 1)]
        send_sem, recv_sem = pair_of_sems(view)
        spread(src_of, dst, n, at, coords, send_sem, recv_sem)
        return lambda: wait_for(view, recv_sem)

    def to_partner(src, dst):
        send_sem, recv_sem = pair_of_sems(dst)
        pltpu.make_async_remote_copy(
            src_ref=src, dst_ref=dst, send_sem=send_sem, recv_sem=recv_sem,
            device_id=(2 * ring_at + 1 - core, row, col), device_id_type=MESH,
        ).start()
        return lambda: wait_for(dst, recv_sem)

    def vis_begin(part, pair):
        return to_partner(part.at[1 - core], pair)

    def vis_middle(arrived, part, pair, ring):
        arrived()
        ring[ring_at] = (part[core].astype(F32) + pair[...].astype(F32)).astype(BF)
        return start(lambda p: ring.at[ring_at], ring, n_ring, ring_at, in_ring)

    def vis_finish(arrived, ring, result):
        arrived()
        value = ring[0].astype(F32)
        for i in range(1, n_ring):
            value = value + ring[i].astype(F32)
        result[core] = value.astype(BF)
        return to_partner(result.at[core], result.at[core])

    def fill(part, value, n, chunk):
        for i in range(n):
            part[i] = value[i * chunk:(i + 1) * chunk].astype(BF)

    def total(recv, part, n, at):
        recv[at] = part[at]
        result = recv[0].astype(F32)
        for i in range(1, n):
            result = result + recv[i].astype(F32)
        return result

    def whole(buf, n):
        return jnp.concatenate([buf[i].astype(F32) for i in range(n)], axis=0)

    loads["images"].wait()
    loads["gain"].wait()
    gain_row = gain[...].reshape(1, gain.shape[0])
    values = images[...].astype(F32)
    centred = values - jnp.mean(values, axis=-1, keepdims=True)
    inverse_scale = lax.rsqrt(jnp.mean(centred * centred, axis=-1, keepdims=True) + 1e-05)
    normed = centred * inverse_scale * gain_row
    for i in range(n_vis):
        blocks[i] = normed[:, i * vf:(i + 1) * vf].astype(BF)
    for name in ("cot", "bias", "counts", "order"):
        loads[name].wait()
    pl.semaphore_wait(barrier, n_dev - 1)
    cot_done = start(lambda p: cot, cot_all, group, pos, in_group)
    mates, own = n_row * n_vis, row * n_vis + vis
    row_steps = sorted(range(n_row), key=lambda k: min(k, n_row - k))
    mates_view = rows_all.at[pl.ds(0, mates - 1)]
    send_sem, _ = pair_of_sems(mates_view)
    spread(
        lambda p: blocks.at[lax.rem(p, n_vis)], rows_all, mates, own, in_column,
        send_sem, gather_sems.at[row], slab=me,
    )
    cot_all[pos] = cot[...]
    rows_all[me] = blocks[vis]
    forward_view = rows_all.at[pl.ds(0, mates * (n_col - 1))]
    forward_send, forward_recv = pair_of_sems(forward_view)

    def forward(k):
        r = lax.rem(row + k, n_row)
        wait_for(rows_all.at[pl.ds(0, n_vis - 1 if k == 0 else n_vis)], gather_sems.at[r])
        chunk = rows_all.at[pl.ds((r * n_col + col) * n_vis, n_vis)]
        for j in range(1, n_col):
            pltpu.make_async_remote_copy(
                src_ref=chunk, dst_ref=chunk, send_sem=forward_send, recv_sem=forward_recv,
                device_id=(vis, row, lax.rem(col + j, n_col)), device_id_type=MESH,
            ).start()

    cot_done()
    upstream[...] = whole(cot_all, group).astype(BF)
    loads["wd"].wait()
    steps_left = list(row_steps)
    for t in range(TILES):
        if steps_left:
            forward(steps_left.pop(0))
        cols = slice(t * tw, (t + 1) * tw)
        value = dot_nt(upstream[...], wd[cols, :])
        for i in range(2):
            h_part[i, :, cols] = value[i * hr:(i + 1) * hr].astype(BF)
    for k in steps_left:
        forward(k)
    h_done = vis_begin(h_part, h_pair)
    n_slots = n_dev * per
    place = row_places(counts, order, n_vis, per, (rows, n_slots), 1)
    pick = jnp.where(place == lax.broadcasted_iota(jnp.int32, (rows, n_slots), 0), 1.0, 0.0).astype(BF)

    loads["wf"].wait()
    wait_for(forward_view, forward_recv)
    packed_out[...] = jnp.dot(
        pick, rows_all[...].reshape(n_slots, vf), preferred_element_type=F32
    ).astype(BF)
    fill(b_part, jnp.dot(packed_out[...], wf[...], preferred_element_type=F32), 2, hr)
    b_done = vis_begin(b_part, b_pair)
    b_done = vis_middle(b_done, b_part, b_pair, b_ring)
    h_done = vis_middle(h_done, h_part, h_pair, h_ring)
    b_done = vis_finish(b_done, b_ring, b_all)
    b_done()
    pre = whole(b_all, 2) + bias[...].reshape(1, bias.shape[0])
    activated, slope_value = gelu_parts(pre)
    slope[...] = slope_value
    hid_out[...] = activated.astype(BF)

    loads["ws"].wait()
    fill(c_part, jnp.dot(hid_out[...], ws[...], preferred_element_type=F32), group, gr)
    c_done = start(lambda p: c_part.at[p], c_recv, group, pos, in_group)
    h_done = vis_finish(h_done, h_ring, h_all)
    c_done()
    c_all[pos] = total(c_recv, c_part, group, pos).astype(BF)
    c_done = start(lambda p: c_all.at[pos], c_all, group, pos, in_group)
    loads["wg"].wait()
    loads["wu"].wait()
    h_done()
    c_done()
    inputs[...] = whole(c_all, group).astype(BF)

    d_done = [None] * TILES
    for t in range(TILES):
        cols = slice(t * tw, (t + 1) * tw)
        for half, weight in enumerate((wg, wu)):
            value = jnp.dot(inputs[...], weight[:, cols], preferred_element_type=F32)
            for i in range(2):
                d_part[t, i, :, half * tw:(half + 1) * tw] = value[i * hr:(i + 1) * hr].astype(BF)
        d_done[t] = vis_begin(d_part.at[t], d_pair.at[t])
        if t > 0:
            d_done[t - 1] = vis_middle(d_done[t - 1], d_part.at[t - 1], d_pair.at[t - 1], d_ring.at[t - 1])
    d_done[-1] = vis_middle(d_done[-1], d_part.at[TILES - 1], d_pair.at[TILES - 1], d_ring.at[TILES - 1])
    d_done[0] = vis_finish(d_done[0], d_ring.at[0], d_all.at[0])
    for t in range(TILES):
        if t + 1 < TILES:
            d_done[t + 1] = vis_finish(d_done[t + 1], d_ring.at[t + 1], d_all.at[t + 1])
        d_done[t]()
        cols = slice(t * tw, (t + 1) * tw)
        both = whole(d_all.at[t], 2)
        gate_sum, up_sum = both[:, :tw], both[:, tw:]
        hidden_grad = jnp.concatenate([h_all[i, :, cols].astype(F32) for i in range(2)], axis=0)
        gate_sigmoid = jax.nn.sigmoid(gate_sum)
        hidden[:, cols] = (gate_sum * gate_sigmoid * up_sum).astype(BF)
        gate_grad, up_grad = feed_grads(hidden_grad, gate_sum, up_sum, gate_sigmoid)
        value = dot_nt(gate_grad, wg[:, cols]) + dot_nt(up_grad, wu[:, cols])
        if t == 0:
            acc[...] = value
        else:
            acc[...] += value
    fill(e_part, acc[...], group, gr)
    e_done = start(lambda p: e_part.at[p], e_recv, group, pos, in_group)

    fill(o_part, jnp.dot(hidden[...], wd[...], preferred_element_type=F32), group, gr)
    e_done()
    e_all[pos] = (total(e_recv, e_part, group, pos) + cot[...].astype(F32)).astype(BF)
    e_done = start(lambda p: e_all.at[pos], e_all, group, pos, in_group)
    o_done = start(lambda p: o_part.at[p], o_recv, group, pos, in_group)
    place = row_places(counts, order, n_vis, per, (n_slots, rows), 0)
    put = jnp.where(place == lax.broadcasted_iota(jnp.int32, (n_slots, rows), 1), 1.0, 0.0).astype(BF)
    e_done()
    ig_out[...] = whole(e_all, group).astype(BF)
    fill(f_part, dot_nt(ig_out[...], ws[...]), 2, hr)
    f_done = vis_begin(f_part, f_pair)
    f_done = vis_middle(f_done, f_part, f_pair, f_ring)
    o_done()
    block_out[...] = (c_all[pos].astype(F32) + total(o_recv, o_part, group, pos)).astype(BF)
    f_done = vis_finish(f_done, f_ring, f_all)
    f_done()
    act_out[...] = (whole(f_all, 2) * slope[...]).astype(BF)

    slot_act = jnp.dot(put, act_out[...], preferred_element_type=F32).astype(BF)
    slabs[...] = dot_nt(slot_act, wf[...]).astype(BF).reshape(n_dev, per, vf)
    across_send, _ = pair_of_sems(slabs.at[pl.ds(0, mates * (n_col - 1))])
    returned_view = returned.at[pl.ds(0, mates - 1)]
    back_send, back_recv = pair_of_sems(returned_view)
    back_steps = row_steps[::-1]
    for k in back_steps:
        r = lax.rem(row + k, n_row)
        for j in range(1, n_col):
            other = lax.rem(col + j, n_col)
            pltpu.make_async_remote_copy(
                src_ref=slabs.at[pl.ds((r * n_col + other) * n_vis, n_vis)],
                dst_ref=across.at[r, col], send_sem=across_send, recv_sem=return_sems.at[r],
                device_id=(vis, row, other), device_id_type=MESH,
            ).start()
    for k in back_steps:
        r = lax.rem(row + k, n_row)
        across[r, col] = slabs[pl.ds((r * n_col + col) * n_vis, n_vis)]
        wait_for(across.at[0, pl.ds(0, n_col - 1)], return_sems.at[r])
        value = across[r, 0].astype(F32)
        for c in range(1, n_col):
            value = value + across[r, c].astype(F32)
        column_sums[r] = value.astype(BF)
        for j in range(1 if k == 0 else 0, n_vis):
            other = lax.rem(vis + j, n_vis)
            pltpu.make_async_remote_copy(
                src_ref=column_sums.at[r, other], dst_ref=returned.at[own],
                send_sem=back_send, recv_sem=back_recv,
                device_id=(other, r, col), device_id_type=MESH,
            ).start()
    returned[own] = column_sums[row, vis]
    wait_for(returned_view, back_recv)
    pieces = []
    for i in range(n_vis):
        value = returned[i].astype(F32)
        for r in range(1, n_row):
            value = value + returned[r * n_vis + i].astype(F32)
        pieces.append(value)
    standardized_input = centred * inverse_scale
    slot_out[...] = norm_gradient_pass(
        jnp.concatenate(pieces, axis=1), standardized_input, inverse_scale, gain_row
    )
    for view, sem in sent:
        wait_for(view, sem)


def vis_buffers(n_vis, lead, half_rows, width):
    return [
        pltpu.VMEM(lead + (2, half_rows, width), BF),
        pltpu.VMEM(lead + (half_rows, width), BF),
        pltpu.VMEM(lead + (n_vis // 2, half_rows, width), BF),
        pltpu.VMEM(lead + (2, half_rows, width), BF),
    ]


def on_device(
    sizes,
    images,
    counts,
    block_order,
    projector_norm_gain,
    proj_first,
    proj_bias,
    proj_second,
    gate_weight,
    up_weight,
    down_weight,
    cotangent,
):
    n_vis, n_row, n_col = sizes
    group_size = n_row * n_col
    n_dev = n_vis * group_size
    per_device = images.shape[0]
    local_rows = cotangent.shape[0]
    rows = local_rows * group_size
    vf, units = proj_first.shape
    dl, ffl = gate_weight.shape
    hr = rows // 2
    by_group = pltpu.VMEM((group_size, local_rows, dl), BF)
    by_device = pltpu.VMEM((n_dev, per_device, vf), BF)
    n_sends = 3 * (3 + TILES) + 5 + 5
    block_out, image_slot_gradients, packed, act_grad, hidden_proj, input_grad = pl.pallas_call(
        functools.partial(chain_kernel, sizes),
        out_shape=(
            jax.ShapeDtypeStruct((local_rows, dl), BF),
            jax.ShapeDtypeStruct(images.shape, F32),
            jax.ShapeDtypeStruct((rows, vf), BF),
            jax.ShapeDtypeStruct((rows, units), BF),
            jax.ShapeDtypeStruct((rows, units), BF),
            jax.ShapeDtypeStruct((rows, dl), BF),
        ),
        in_specs=[ANY] * 11,
        out_specs=(VM,) * 6,
        scratch_shapes=[
            pltpu.SMEM(counts.shape, jnp.int32),
            pltpu.SMEM(block_order.shape, jnp.int32),
            pltpu.VMEM(images.shape, BF),
            pltpu.VMEM(projector_norm_gain.shape, F32),
            pltpu.VMEM(cotangent.shape, BF),
            pltpu.VMEM(proj_bias.shape, F32),
            pltpu.VMEM(proj_first.shape, BF),
            pltpu.VMEM(proj_second.shape, BF),
            pltpu.VMEM(gate_weight.shape, BF),
            pltpu.VMEM(up_weight.shape, BF),
            pltpu.VMEM(down_weight.shape, BF),
            pltpu.VMEM((n_vis, per_device, vf), BF),
            by_device,
            by_group,
            pltpu.VMEM((rows, dl), BF),
            by_device,
            pltpu.VMEM((n_row, n_col, n_vis, per_device, vf), BF),
            pltpu.VMEM((n_row, n_vis, per_device, vf), BF),
            pltpu.VMEM((n_row * n_vis, per_device, vf), BF),
            *vis_buffers(n_vis, (), hr, units),
            *vis_buffers(n_vis, (), hr, ffl),
            *vis_buffers(n_vis, (TILES,), hr, 2 * ffl // TILES),
            *vis_buffers(n_vis, (), hr, units),
            *[by_group] * 8,
            pltpu.VMEM((rows, units), F32),
            pltpu.VMEM((rows, dl), BF),
            pltpu.VMEM((rows, dl), F32),
            pltpu.VMEM((rows, ffl), BF),
            pltpu.SemaphoreType.DMA((11,)),
            pltpu.SemaphoreType.DMA((n_row,)),
            pltpu.SemaphoreType.DMA((n_row,)),
            pltpu.SemaphoreType.DMA((2 * n_sends,)),
        ],
        compiler_params=pltpu.CompilerParams(
            collective_id=0, has_side_effects=True, vmem_limit_bytes=48 << 20
        ),
    )(
        counts, block_order, images, projector_norm_gain, cotangent,
        proj_bias, proj_first, proj_second, gate_weight, up_weight, down_weight,
    )
    second_grad = product(hidden_proj.T, input_grad)
    first_grad = product(packed.T, act_grad)
    return (block_out, image_slot_gradients, first_grad, second_grad)


def solution(mesh):
    in_specs = (
        P(("vis", "row", "col"), None),
        P(),
        P(),
        P(),
        P("vis", ("row", "col")),
        P(("row", "col")),
        P(("row", "col"), "vis"),
        P("vis", ("row", "col")),
        P("vis", ("row", "col")),
        P(("row", "col"), "vis"),
        P(("row", "col"), "vis"),
    )
    out_specs = (
        P(("row", "col"), "vis"),
        P(("vis", "row", "col"), None),
        P("vis", ("row", "col")),
        P(("row", "col"), "vis"),
    )
    sizes = (mesh.shape["vis"], mesh.shape["row"], mesh.shape["col"])
    return jax.shard_map(
        functools.partial(on_device, sizes), mesh=mesh, in_specs=in_specs, out_specs=out_specs, check_vma=False
    )
```
